32 devices in a mesh: grp: 2 (over x), smp: 16 (over z, y, core).
Axes of the slice: x: 2, y: 2, z: 4, core: 2. Of those that a mesh axis runs over, the one named last changes fastest.
Arguments:
- dosage: bfloat16 [2048, 4096], P('smp', 'grp'), parts along dimension 1, may hold values from 0.008 to 4.5, as said below
- flags: int32 [256], P('grp'), parts along dimension 0, may hold values from 0 to 2047, as said below
- events: int32 [2048, 32], P('smp', 'grp'), parts along dimension 1, may hold values from 0 to 1, as said below
- offsets: float32 [2048, 32], P('smp', 'grp'), parts along dimension 1, may hold values from -3 to 3
Outputs:
- effect: float32 [16, 256], P(None, 'grp'), parts along dimension 1
- zscore: float32 [16, 256], P(None, 'grp'), parts along dimension 1
The draws below stay inside these ranges and needn't reach their ends.
There are 2 independent parts, one for each index of `grp`. The reference program is written for one: setup_inputs(seed, part) draws one part's arguments, and reference() takes and returns one part's arrays. A program takes and returns all parts, laid end to end along the dimension named above; each array names one. Nothing has to cross between parts.
Inputs may be any that keep to these rules, and one draw needn't show every extreme that they name: `flags`: 128 distinct column numbers in rising order, the first 0 and the last 2047. `events`: 0 or 1; every endpoint has an event at the first sample. `dosage`: positive dosages.
All inputs are finite; a program needn't handle non-finite values.
Results may differ from the reference program's by a relative error of at most 0.0013.
Values sent between devices are 32-bit elements; how exact they have to be, the bound alone decides.
A program may use at most 64 MiB of HBM per device.

```python
import jax
import jax.numpy as jnp
from jax import lax

E = 16
V = 128
C = 2048
ITERS = 3
N = 2048


def draw_flags(key, part):
    middle = jax.random.permutation(key, jnp.arange(1, C - 1, dtype=jnp.int32))[:V - 2]
    chosen = jnp.concatenate([jnp.zeros((1,), jnp.int32), middle.astype(jnp.int32), jnp.full((1,), C - 1, jnp.int32)])
    return jnp.sort(chosen).astype(jnp.int32)


def event_table(key):
    picks = jax.random.randint(jax.random.fold_in(key, 11), (N, E), 0, 16)
    marked = (picks == 0).astype(jnp.int32)
    first_row = (jnp.arange(N, dtype=jnp.int32) == 0).astype(jnp.int32)[:, None]
    return jnp.maximum(marked, first_row).astype(jnp.int32)


def draw_events(key, part):
    return event_table(key)


def draw_dosage(key, part):
    marked = event_table(key).astype(jnp.float32)
    key_base = jax.random.fold_in(key, 21)
    key_link = jax.random.fold_in(key, 22)
    key_sign = jax.random.fold_in(key, 23)
    key_level = jax.random.fold_in(key, 24)
    base = jnp.exp(jax.random.uniform(key_base, (N, C), jnp.float32, jnp.log(0.02), jnp.log(2.0)))
    linked = jax.random.randint(key_link, (C,), 0, E)
    signs = (2 * jax.random.randint(key_sign, (C,), 0, 2) - 1).astype(jnp.float32)
    strength = jax.random.uniform(key_level, (C,), jnp.float32, 0.3, 0.8) * signs
    chosen = jnp.take(marked, linked, axis=1)
    return (base * jnp.exp(strength[None, :] * chosen)).astype(jnp.bfloat16)


def shard_levels(stream_key, extent, cuts, smallest, largest):
    level = 1.0
    for axis_at, parts in cuts:
        steps = jax.random.uniform(jax.random.fold_in(jax.random.fold_in(stream_key, 6), axis_at), (parts,), jnp.float32, smallest / len(cuts), largest / len(cuts))
        level = level * jnp.repeat(jnp.exp(steps), extent[axis_at] // parts).reshape((-1,) + (1,) * (len(extent) - 1 - axis_at))
    return level


def scatter_about(stream_key, shape, spread, limit, shards=(), kind=jnp.bfloat16):
    drawn = spread * jax.random.normal(stream_key, shape, jnp.float32)
    if shards:
        drawn = drawn * shard_levels(stream_key, shape, shards, -0.22, 0.18)
    return jnp.clip(drawn, -limit, limit).astype(kind)


def setup_inputs(seed: int = 0, part: int = 0) -> dict:
    splits = jax.random.split(jax.random.key(seed), 5)
    part_keys = jax.random.split(jax.random.fold_in(splits[4], part), 5)
    return {
        "dosage": draw_dosage(jax.random.fold_in(jax.random.fold_in(splits[4], part), 71), part),
        "flags": draw_flags(jax.random.fold_in(jax.random.fold_in(splits[4], part), 71), part),
        "events": draw_events(jax.random.fold_in(jax.random.fold_in(splits[4], part), 71), part),
        "offsets": scatter_about(part_keys[3], (N, E), 0.5, 3.0, ((0, 16),), jnp.float32),
    }


def reference(dosage, flags, events, offsets):
    genotype = jnp.take(dosage, flags, axis=1).astype(jnp.float32)

    def fit_endpoint(inputs):
        hazard_offset, indicator = inputs
        effect = jnp.zeros((genotype.shape[1],), jnp.float32)
        zscore = effect
        dose = genotype
        for sweep in range(ITERS):
            weight = jnp.exp(hazard_offset[:, None] + effect[None, :] * dose)
            moments = jnp.stack([weight, weight * dose, weight * dose * dose, weight * dose * dose * dose])
            suffix = lax.cumsum(moments, axis=1, reverse=True)
            first = suffix[1] / suffix[0]
            second = suffix[2] / suffix[0]
            third = suffix[3] / suffix[0]
            mark = indicator[:, None]
            score = lax.optimization_barrier(jnp.sum(mark * (dose - first), axis=0))
            information = lax.optimization_barrier(jnp.sum(mark * (second - first * first), axis=0))
            skewness = lax.optimization_barrier(jnp.sum(mark * (third - 3.0 * first * second + 2.0 * first * first * first), axis=0))
            effect = effect + (score + 0.5 * skewness / information) / information
            zscore = effect * jnp.sqrt(information)
        return (effect, zscore)
    effect, zscore = lax.map(fit_endpoint, (offsets.T, events.T.astype(jnp.float32)))
    return (effect, zscore)
```

```python
import functools

import jax
import jax.numpy as jnp
from jax import lax
from jax.experimental import pallas as pl
from jax.experimental.pallas import tpu as pltpu
from jax.sharding import PartitionSpec as P

ITERS = 3
SUB = 8
MESH = pl.DeviceIdType.MESH
F32 = jnp.float32
BF16 = jnp.bfloat16


def thirds(x):
    high = x.astype(BF16).astype(F32)
    rest = x - high
    middle = rest.astype(BF16).astype(F32)
    return high, middle, rest - middle


def transposed_dot(a, b):
    return lax.dot_general(a, b, (((0,), (0,)), ((), ())), preferred_element_type=F32)


def iota(shape, dim):
    return lax.broadcasted_iota(jnp.int32, shape, dim)


def kernel(
    n, flags_hbm, dosage_hbm, offsets_hbm, events_hbm, effect_ref, zscore_ref,
    flags_ref, dosage_ref, offsets_ref, events_ref,
    gsend, osend, grecv, orecv, dose_ref, shift_ref, mark_ref, weight_ref, totals, carries, rsend, rrecv,
    load_sem, gsend_sem, grecv_sem, osend_sem, orecv_sem, rsend_sem, rrecv_sem,
):
    me = lax.axis_index("smp")
    rows, columns = dosage_ref.shape
    endpoints = offsets_ref.shape[1]
    variants = flags_ref.shape[1]
    own = variants // n
    lanes = dose_ref.shape[1]
    steps = rows // SUB

    loads = [
        pltpu.make_async_copy(src, dst, load_sem.at[at])
        for at, (src, dst) in enumerate(
            ((flags_hbm, flags_ref), (dosage_hbm, dosage_ref), (offsets_hbm, offsets_ref), (events_hbm, events_ref))
        )
    ]
    for load in loads:
        load.start()

    barrier = pltpu.get_barrier_semaphore()

    def peer(step):
        return lax.rem(me + step, n)

    @pl.loop(1, n)
    def _(step):
        pl.semaphore_signal(barrier, inc=1, device_id={"smp": peer(step)}, device_id_type=MESH)

    line = iota((rows, rows), 1)
    order = (iota((rows, rows), 0) == lax.rem(line, SUB) * steps + lax.div(line, SUB)).astype(F32).astype(BF16)

    loads[2].wait()
    loads[3].wait()
    three = [transposed_dot(part.astype(BF16), order) for part in thirds(offsets_ref[...])]
    osend[pl.ds(0, endpoints), :] = (three[0] + three[1]) + three[2]
    osend[pl.ds(endpoints, endpoints), :] = transposed_dot(events_ref[...].astype(F32).astype(BF16), order)

    loads[0].wait()
    loads[1].wait()
    chosen = (iota((columns, variants), 0) == flags_ref[...]).astype(F32).astype(BF16)
    genotype = jnp.dot(dosage_ref[...], chosen, preferred_element_type=F32).astype(BF16)
    gsend[...] = transposed_dot(genotype, order).reshape(n, own, rows)

    pl.semaphore_wait(barrier, n - 1)

    def gcopy(at, slot):
        return pltpu.make_async_remote_copy(
            src_ref=gsend.at[at], dst_ref=grecv.at[slot], send_sem=gsend_sem.at[at], recv_sem=grecv_sem.at[slot],
            device_id={"smp": at}, device_id_type=MESH,
        )

    def ocopy(at, slot):
        return pltpu.make_async_remote_copy(
            src_ref=osend, dst_ref=orecv.at[slot], send_sem=osend_sem.at[at], recv_sem=orecv_sem.at[slot],
            device_id={"smp": at}, device_id_type=MESH,
        )

    def rcopy(at, slot):
        return pltpu.make_async_remote_copy(
            src_ref=rsend, dst_ref=rrecv.at[slot], send_sem=rsend_sem.at[at], recv_sem=rrecv_sem.at[slot],
            device_id={"smp": at}, device_id_type=MESH,
        )

    @pl.loop(1, n)
    def _(step):
        ocopy(peer(step), me).start()
        gcopy(peer(step), me).start()

    lane_e = iota((endpoints, lanes), 1)
    spread_e = (lax.div(lane_e, own) == iota((endpoints, lanes), 0)).astype(F32).astype(BF16)
    lane_v = iota((own, lanes), 1)
    spread_v = jnp.logical_and(lax.rem(lane_v, own) == iota((own, lanes), 0), lane_v < own * endpoints)
    spread_v = spread_v.astype(F32).astype(BF16)

    def expand(slot, doses, samples):
        at = pl.ds(pl.multiple_of(slot * rows, rows), rows)
        dose_ref[at, :] = transposed_dot(doses.astype(BF16), spread_v)
        parts = [transposed_dot(part.astype(BF16), spread_e) for part in thirds(samples[:endpoints])]
        shift_ref[at, :] = (parts[0] + parts[1]) + parts[2]
        mark_ref[at, :] = transposed_dot(samples[endpoints:].astype(BF16), spread_e)

    expand(me, gsend[me], osend[...])

    @pl.loop(1, n)
    def _(step):
        slot = peer(step)
        ocopy(slot, slot).wait_recv()
        gcopy(slot, slot).wait_recv()
        expand(slot, grecv[slot], orecv[slot])

    blocks = n * SUB
    after = (iota((blocks, blocks), 1) > iota((blocks, blocks), 0)).astype(F32).astype(BF16)
    effect = jnp.zeros((1, lanes), F32)
    zscore = effect
    for sweep in range(ITERS):
        slope = jnp.broadcast_to(effect, (SUB, lanes))

        def add_up(block, _):
            sums = [jnp.zeros((SUB, lanes), F32)] * 4
            for t in range(steps):
                at = pl.ds(pl.multiple_of(block * rows + t * SUB, SUB), SUB)
                dose = dose_ref[at, :]
                moment = jnp.exp(shift_ref[at, :] + slope * dose)
                weight_ref[at, :] = moment
                for k in range(4):
                    sums[k] = sums[k] + moment
                    if k < 3:
                        moment = moment * dose
            for k in range(4):
                totals[pl.ds(pl.multiple_of(block * SUB, SUB), SUB), pl.ds(k * lanes, lanes)] = sums[k]
            return 0

        lax.fori_loop(0, n, add_up, 0, unroll=2)
        parts = [
            jnp.dot(after, part.astype(BF16), preferred_element_type=F32) for part in thirds(totals[...])
        ]
        carries[...] = (parts[0] + parts[1]) + parts[2]

        def add_terms(block, sums):
            score, information, skewness = sums
            here = pl.ds(pl.multiple_of(block * SUB, SUB), SUB)
            suffix = [carries[here, pl.ds(k * lanes, lanes)] for k in range(4)]
            for t in reversed(range(steps)):
                at = pl.ds(pl.multiple_of(block * rows + t * SUB, SUB), SUB)
                dose = dose_ref[at, :]
                mark = mark_ref[at, :]
                moment = weight_ref[at, :]
                for k in range(4):
                    suffix[k] = suffix[k] + moment
                    if k < 3:
                        moment = moment * dose
                inverse = 1.0 / suffix[0]
                first = suffix[1] * inverse
                second = suffix[2] * inverse
                third = suffix[3] * inverse
                spread = second - first * first
                score = score + mark * (dose - first)
                information = information + mark * spread
                skewness = skewness + mark * (third - first * (second + (spread + spread)))
            return score, information, skewness

        zero = jnp.zeros((SUB, lanes), F32)
        sums = lax.fori_loop(0, n, add_terms, (zero, zero, zero), unroll=2)
        score, information, skewness = (jnp.sum(x, axis=0, keepdims=True) for x in sums)
        effect = effect + (score + 0.5 * skewness / information) / information
        zscore = effect * jnp.sqrt(information)

    rsend[0:1, :] = effect
    rsend[1:2, :] = zscore

    @pl.loop(1, n)
    def _(step):
        rcopy(peer(step), me).start()

    rrecv[me] = rsend[...]

    @pl.loop(1, n)
    def _(step):
        gcopy(peer(step), me).wait_send()
        ocopy(peer(step), me).wait_send()

    @pl.loop(1, n)
    def _(step):
        rcopy(peer(step), peer(step)).wait_recv()

    owner = lax.div(iota((endpoints, lanes), 1), own) == iota((endpoints, lanes), 0)
    fold = jnp.logical_and(
        lax.rem(iota((lanes, variants), 0), own) == lax.rem(iota((lanes, variants), 1), own),
        iota((lanes, variants), 0) < own * endpoints,
    ).astype(F32).astype(BF16)
    column = lax.div(iota((endpoints, variants), 1), own)
    for which, out in enumerate((effect_ref, zscore_ref)):
        tall = jnp.concatenate([jnp.where(owner, rrecv[k, which : which + 1, :], 0.0) for k in range(n)], axis=0)
        parts = [jnp.dot(part.astype(BF16), fold, preferred_element_type=F32) for part in thirds(tall)]
        tall = (parts[0] + parts[1]) + parts[2]
        result = jnp.zeros((endpoints, variants), F32)
        for k in range(n):
            result = jnp.where(column == k, tall[k * endpoints : (k + 1) * endpoints], result)
        out[...] = result

    @pl.loop(1, n)
    def _(step):
        rcopy(peer(step), me).wait_send()


def solution(mesh):
    n = mesh.shape["smp"]

    def body(dosage, flags, events, offsets):
        rows, columns = dosage.shape
        endpoints = offsets.shape[1]
        variants = flags.shape[0]
        own = variants // n
        lanes = -(-own * endpoints // 128) * 128
        out = jax.ShapeDtypeStruct((endpoints, variants), F32)
        return pl.pallas_call(
            functools.partial(kernel, n),
            out_shape=(out, out),
            in_specs=[pl.BlockSpec(memory_space=pl.ANY)] * 4,
            out_specs=[pl.BlockSpec(memory_space=pltpu.VMEM)] * 2,
            scratch_shapes=[
                pltpu.VMEM((1, variants), jnp.int32),
                pltpu.VMEM((rows, columns), BF16),
                pltpu.VMEM((rows, endpoints), F32),
                pltpu.VMEM((rows, endpoints), jnp.int32),
                pltpu.VMEM((n, own, rows), F32),
                pltpu.VMEM((2 * endpoints, rows), F32),
                pltpu.VMEM((n, own, rows), F32),
                pltpu.VMEM((n, 2 * endpoints, rows), F32),
                pltpu.VMEM((n * rows, lanes), F32),
                pltpu.VMEM((n * rows, lanes), F32),
                pltpu.VMEM((n * rows, lanes), F32),
                pltpu.VMEM((n * rows, lanes), F32),
                pltpu.VMEM((n * SUB, 4 * lanes), F32),
                pltpu.VMEM((n * SUB, 4 * lanes), F32),
                pltpu.VMEM((2, lanes), F32),
                pltpu.VMEM((n, 2, lanes), F32),
                pltpu.SemaphoreType.DMA((4,)),
            ]
            + [pltpu.SemaphoreType.DMA((n,))] * 6,
            compiler_params=pltpu.CompilerParams(collective_id=0, has_side_effects=True),
        )(flags.reshape(1, variants), dosage, offsets, events)

    return jax.shard_map(
        body,
        mesh=mesh,
        in_specs=(P("smp", "grp"), P("grp"), P("smp", "grp"), P("smp", "grp")),
        out_specs=(P(None, "grp"), P(None, "grp")),
        check_vma=False,
    )
```

```python
import functools

import jax
import jax.numpy as jnp
from jax import lax
from jax.experimental import pallas as pl
from jax.experimental.pallas import tpu as pltpu
from jax.sharding import PartitionSpec as P

ITERS = 3
SUB = 8
MESH = pl.DeviceIdType.MESH
F32 = jnp.float32
BF16 = jnp.bfloat16


def thirds(x):
    high = x.astype(BF16).astype(F32)
    rest = x - high
    middle = rest.astype(BF16).astype(F32)
    return high, middle, rest - middle


def transposed_dot(a, b):
    return lax.dot_general(a, b, (((0,), (0,)), ((), ())), preferred_element_type=F32)


def iota(shape, dim):
    return lax.broadcasted_iota(jnp.int32, shape, dim)


def kernel(
    n, flags_hbm, dosage_hbm, offsets_hbm, events_hbm, effect_ref, zscore_ref,
    flags_ref, dosage_ref, offsets_ref, events_ref,
    gsend, osend, grecv, orecv, dose_ref, shift_ref, mark_ref, weight_ref, totals, carries, rsend, rrecv,
    load_sem, gsend_sem, grecv_sem, osend_sem, orecv_sem, rsend_sem, rrecv_sem,
):
    me = lax.axis_index("smp")
    rows, columns = dosage_ref.shape
    endpoints = offsets_ref.shape[0]
    variants = flags_ref.shape[1]
    own = variants // n
    lanes = dose_ref.shape[1]
    steps = rows // SUB

    loads = [
        pltpu.make_async_copy(src, dst, load_sem.at[at])
        for at, (src, dst) in enumerate(
            ((flags_hbm, flags_ref), (dosage_hbm, dosage_ref), (offsets_hbm, offsets_ref), (events_hbm, events_ref))
        )
    ]
    for load in loads:
        load.start()

    barrier = pltpu.get_barrier_semaphore()

    def peer(step):
        return lax.rem(me + step, n)

    @pl.loop(1, n)
    def _(step):
        pl.semaphore_signal(barrier, inc=1, device_id={"smp": peer(step)}, device_id_type=MESH)

    line = iota((rows, rows), 1)
    order = (iota((rows, rows), 0) == lax.rem(line, SUB) * steps + lax.div(line, SUB)).astype(F32).astype(BF16)

    loads[2].wait()
    loads[3].wait()
    four = jnp.concatenate([*thirds(offsets_ref[...]), events_ref[...].astype(F32)], axis=0)
    four = jnp.dot(four.astype(BF16), order, preferred_element_type=F32)
    high, middle, low, events = (four[k * endpoints : (k + 1) * endpoints] for k in range(4))
    osend[pl.ds(0, endpoints), :] = (high + middle) + low
    osend[pl.ds(endpoints, endpoints), :] = events

    loads[0].wait()
    chosen = (iota((columns, variants), 0) == flags_ref[...]).astype(F32).astype(BF16)
    loads[1].wait()
    genotype = jnp.dot(dosage_ref[...], chosen, preferred_element_type=F32).astype(BF16)
    gsend[...] = transposed_dot(genotype, order).reshape(n, own, rows)

    pl.semaphore_wait(barrier, n - 1)

    def gcopy(at, slot):
        return pltpu.make_async_remote_copy(
            src_ref=gsend.at[at], dst_ref=grecv.at[slot], send_sem=gsend_sem.at[at], recv_sem=grecv_sem.at[slot],
            device_id={"smp": at}, device_id_type=MESH,
        )

    def ocopy(at, slot, src=osend, relayed=0):
        mark = n + slot if relayed else at
        return pltpu.make_async_remote_copy(
            src_ref=src, dst_ref=orecv.at[slot], send_sem=osend_sem.at[mark], recv_sem=orecv_sem.at[slot],
            device_id={"smp": at}, device_id_type=MESH,
        )

    def rcopy(at, slot):
        return pltpu.make_async_remote_copy(
            src_ref=rsend, dst_ref=rrecv.at[slot], send_sem=rsend_sem.at[at], recv_sem=rrecv_sem.at[slot],
            device_id={"smp": at}, device_id_type=MESH,
        )

    half = lax.rem(me, 2)
    other = me + 1 - 2 * half

    def chip(step):
        return lax.rem(me - half + 2 * step + n, n)

    ocopy(other, me).start()
    gcopy(other, me).start()

    @pl.loop(1, n // 2)
    def _(step):
        at = chip(step)
        ocopy(at + half, me).start()
        gcopy(at + half, me).start()
        gcopy(at + 1 - half, me).start()

    lane_e = iota((endpoints, lanes), 1)
    lane_v = iota((own, lanes), 1)
    spread_e = (lax.div(lane_e, own) == iota((endpoints, lanes), 0)).astype(F32)
    spread_v = jnp.logical_and(lax.rem(lane_v, own) == iota((own, lanes), 0), lane_v < own * endpoints).astype(F32)
    none_e, none_v = jnp.zeros_like(spread_e), jnp.zeros_like(spread_v)
    spread = jnp.concatenate(
        [jnp.concatenate([spread_e, none_e, none_e], axis=1)] * 3
        + [jnp.concatenate([none_e, spread_e, none_e], axis=1), jnp.concatenate([none_v, none_v, spread_v], axis=1)],
        axis=0,
    ).astype(BF16)

    def expand(slot, doses, samples):
        at = pl.ds(pl.multiple_of(slot * rows, rows), rows)
        mixed = jnp.concatenate([*thirds(samples[:endpoints]), samples[endpoints:], doses], axis=0)
        mixed = transposed_dot(mixed.astype(BF16), spread)
        shift_ref[at, :] = mixed[:, :lanes]
        mark_ref[at, :] = mixed[:, lanes : 2 * lanes]
        dose_ref[at, :] = mixed[:, 2 * lanes :]

    expand(me, gsend[me], osend[...])
    ocopy(other, other).wait_recv()
    gcopy(other, other).wait_recv()
    expand(other, grecv[other], orecv[other])

    @pl.loop(1, n // 2)
    def _(step):
        near = chip(-step) + half
        ocopy(near, near).wait_recv()
        ocopy(other, near, orecv.at[near], 1).start()
        gcopy(near, near).wait_recv()
        expand(near, grecv[near], orecv[near])
        @pl.when(step > 1)
        def _():
            late = chip(1 - step) + 1 - half
            ocopy(late, late).wait_recv()
            gcopy(late, late).wait_recv()
            expand(late, grecv[late], orecv[late])

    last = chip(1 - n // 2) + 1 - half
    ocopy(last, last).wait_recv()
    gcopy(last, last).wait_recv()
    expand(last, grecv[last], orecv[last])

    blocks = n * SUB
    after = (iota((blocks, blocks), 1) > iota((blocks, blocks), 0)).astype(F32).astype(BF16)
    effect = jnp.zeros((1, lanes), F32)
    zscore = effect
    for sweep in range(ITERS):
        slope = jnp.broadcast_to(effect, (SUB, lanes))

        def add_up(block, _):
            sums = [jnp.zeros((SUB, lanes), F32)] * 4
            for t in range(steps):
                at = pl.ds(pl.multiple_of(block * rows + t * SUB, SUB), SUB)
                dose = dose_ref[at, :]
                moment = jnp.exp(shift_ref[at, :] + slope * dose)
                weight_ref[at, :] = moment
                for k in range(4):
                    sums[k] = sums[k] + moment
                    if k < 3:
                        moment = moment * dose
            for k in range(4):
                totals[pl.ds(pl.multiple_of(block * SUB, SUB), SUB), pl.ds(k * lanes, lanes)] = sums[k]
            return 0

        lax.fori_loop(0, n, add_up, 0, unroll=2)
        parts = [
            jnp.dot(after, part.astype(BF16), preferred_element_type=F32) for part in thirds(totals[...])
        ]
        carries[...] = (parts[0] + parts[1]) + parts[2]

        def add_terms(block, sums):
            score, information, skewness = sums
            here = pl.ds(pl.multiple_of(block * SUB, SUB), SUB)
            suffix = [carries[here, pl.ds(k * lanes, lanes)] for k in range(4)]
            for t in reversed(range(steps)):
                at = pl.ds(pl.multiple_of(block * rows + t * SUB, SUB), SUB)
                dose = dose_ref[at, :]
                mark = mark_ref[at, :]
                moment = weight_ref[at, :]
                for k in range(4):
                    suffix[k] = suffix[k] + moment
                    if k < 3:
                        moment = moment * dose
                inverse = 1.0 / suffix[0]
                first = suffix[1] * inverse
                second = suffix[2] * inverse
                third = suffix[3] * inverse
                spread = second - first * first
                score = score + mark * (dose - first)
                information = information + mark * spread
                skewness = skewness + mark * (third - first * (second + (spread + spread)))
            return score, information, skewness

        zero = jnp.zeros((SUB, lanes), F32)
        sums = lax.fori_loop(0, n, add_terms, (zero, zero, zero), unroll=2)
        score, information, skewness = (jnp.sum(x, axis=0, keepdims=True) for x in sums)
        effect = effect + (score + 0.5 * skewness / information) / information
        zscore = effect * jnp.sqrt(information)

    rsend[0:1, :] = effect
    rsend[1:2, :] = zscore

    @pl.loop(1, n)
    def _(step):
        rcopy(peer(step), me).start()

    rrecv[me] = rsend[...]
    ocopy(other, me).wait_send()

    @pl.loop(1, n // 2)
    def _(step):
        near = chip(step) + half
        ocopy(near, me).wait_send()
        ocopy(other, near, orecv.at[near], 1).wait_send()

    @pl.loop(1, n)
    def _(step):
        gcopy(peer(step), me).wait_send()

    @pl.loop(1, n)
    def _(step):
        rcopy(peer(step), peer(step)).wait_recv()

    owner = lax.div(iota((endpoints, lanes), 1), own) == iota((endpoints, lanes), 0)
    fold = jnp.logical_and(
        lax.rem(iota((lanes, variants), 0), own) == lax.rem(iota((lanes, variants), 1), own),
        iota((lanes, variants), 0) < own * endpoints,
    ).astype(F32).astype(BF16)
    column = lax.div(iota((endpoints, variants), 1), own)
    for which, out in enumerate((effect_ref, zscore_ref)):
        tall = jnp.concatenate([jnp.where(owner, rrecv[k, which : which + 1, :], 0.0) for k in range(n)], axis=0)
        parts = [jnp.dot(part.astype(BF16), fold, preferred_element_type=F32) for part in thirds(tall)]
        tall = (parts[0] + parts[1]) + parts[2]
        result = jnp.zeros((endpoints, variants), F32)
        for k in range(n):
            result = jnp.where(column == k, tall[k * endpoints : (k + 1) * endpoints], result)
        out[...] = result

    @pl.loop(1, n)
    def _(step):
        rcopy(peer(step), me).wait_send()


def solution(mesh):
    n = mesh.shape["smp"]

    def body(dosage, flags, events, offsets):
        rows, columns = dosage.shape
        endpoints = offsets.shape[1]
        variants = flags.shape[0]
        own = variants // n
        lanes = -(-own * endpoints // 128) * 128
        out = jax.ShapeDtypeStruct((endpoints, variants), F32)
        return pl.pallas_call(
            functools.partial(kernel, n),
            out_shape=(out, out),
            in_specs=[pl.BlockSpec(memory_space=pl.ANY)] * 4,
            out_specs=[pl.BlockSpec(memory_space=pltpu.VMEM)] * 2,
            scratch_shapes=[
                pltpu.VMEM((1, variants), jnp.int32),
                pltpu.VMEM((rows, columns), BF16),
                pltpu.VMEM((endpoints, rows), F32),
                pltpu.VMEM((endpoints, rows), jnp.int32),
                pltpu.VMEM((n, own, rows), F32),
                pltpu.VMEM((2 * endpoints, rows), F32),
                pltpu.VMEM((n, own, rows), F32),
                pltpu.VMEM((n, 2 * endpoints, rows), F32),
                pltpu.VMEM((n * rows, lanes), F32),
                pltpu.VMEM((n * rows, lanes), F32),
                pltpu.VMEM((n * rows, lanes), F32),
                pltpu.VMEM((n * rows, lanes), F32),
                pltpu.VMEM((n * SUB, 4 * lanes), F32),
                pltpu.VMEM((n * SUB, 4 * lanes), F32),
                pltpu.VMEM((2, lanes), F32),
                pltpu.VMEM((n, 2, lanes), F32),
                pltpu.SemaphoreType.DMA((4,)),
            ]
            + [pltpu.SemaphoreType.DMA((size,)) for size in (n, n, 2 * n, n, n, n)],
            compiler_params=pltpu.CompilerParams(collective_id=0, has_side_effects=True),
        )(flags.reshape(1, variants), dosage, offsets.T, events.T)

    return jax.shard_map(
        body,
        mesh=mesh,
        in_specs=(P("smp", "grp"), P("grp"), P("smp", "grp"), P("smp", "grp")),
        out_specs=(P(None, "grp"), P(None, "grp")),
        check_vma=False,
    )
```

```python
import functools

import jax
import jax.numpy as jnp
from jax import lax
from jax.experimental import pallas as pl
from jax.experimental.pallas import tpu as pltpu
from jax.sharding import PartitionSpec as P

ITERS = 3
SUB = 8
MESH = pl.DeviceIdType.MESH
F32 = jnp.float32
BF16 = jnp.bfloat16


def thirds(x):
    high = x.astype(BF16).astype(F32)
    rest = x - high
    middle = rest.astype(BF16).astype(F32)
    return high, middle, rest - middle


def transposed_dot(a, b):
    return lax.dot_general(a, b, (((0,), (0,)), ((), ())), preferred_element_type=F32)


def iota(shape, dim):
    return lax.broadcasted_iota(jnp.int32, shape, dim)


def kernel(
    n, flags_hbm, dosage_hbm, offsets_hbm, events_hbm, out_ref,
    flags_ref, dosage_ref, offsets_ref, events_ref,
    send, recv, dose_ref, shift_ref, mark_ref, weight_ref, totals, carries, rsend, rrecv,
    load_sem, send_sem, recv_sem, rsend_sem, rrecv_sem,
):
    me = lax.axis_index("smp")
    rows, columns = dosage_ref.shape
    endpoints = offsets_ref.shape[0]
    part = endpoints // 2
    variants = flags_ref.shape[1]
    own = variants * 2 // n
    lanes = dose_ref.shape[1]
    steps = rows // SUB

    loads = [
        pltpu.make_async_copy(src, dst, load_sem.at[at])
        for at, (src, dst) in enumerate(
            ((flags_hbm, flags_ref), (dosage_hbm, dosage_ref), (offsets_hbm, offsets_ref), (events_hbm, events_ref))
        )
    ]
    for load in loads:
        load.start()

    barrier = pltpu.get_barrier_semaphore()

    def peer(step):
        return lax.rem(me + step, n)

    @pl.loop(1, n)
    def _(step):
        pl.semaphore_signal(barrier, inc=1, device_id={"smp": peer(step)}, device_id_type=MESH)

    line = iota((rows, rows), 1)
    order = (iota((rows, rows), 0) == lax.rem(line, SUB) * steps + lax.div(line, SUB)).astype(F32).astype(BF16)

    loads[2].wait()
    loads[3].wait()
    four = jnp.concatenate([*thirds(offsets_ref[...]), events_ref[...].astype(F32)], axis=0)
    four = jnp.dot(four.astype(BF16), order, preferred_element_type=F32)
    high, middle, low, events = (four[k * endpoints : (k + 1) * endpoints] for k in range(4))
    offsets = (high + middle) + low
    for k in range(n):
        for at, values in ((own, offsets), (own + part, events)):
            send[k, pl.ds(at, part), :] = values[k % 2 * part : (k % 2 + 1) * part]

    loads[0].wait()
    chosen = (iota((columns, variants), 0) == flags_ref[...]).astype(F32).astype(BF16)
    loads[1].wait()
    genotype = jnp.dot(dosage_ref[...], chosen, preferred_element_type=F32).astype(BF16)
    genotype = transposed_dot(genotype, order)
    for k in range(n):
        send[k, pl.ds(0, own), :] = genotype[k // 2 * own : (k // 2 + 1) * own]

    pl.semaphore_wait(barrier, n - 1)

    def copy(at, slot):
        return pltpu.make_async_remote_copy(
            src_ref=send.at[at], dst_ref=recv.at[slot], send_sem=send_sem.at[at], recv_sem=recv_sem.at[slot],
            device_id={"smp": at}, device_id_type=MESH,
        )

    def rcopy(at, slot):
        return pltpu.make_async_remote_copy(
            src_ref=rsend, dst_ref=rrecv.at[slot], send_sem=rsend_sem.at[at], recv_sem=rrecv_sem.at[slot],
            device_id={"smp": at}, device_id_type=MESH,
        )

    @pl.loop(1, n)
    def _(step):
        copy(peer(step), me).start()

    lane_e = iota((part, lanes), 1)
    lane_v = iota((own, lanes), 1)
    spread_e = (lax.div(lane_e, own) == iota((part, lanes), 0)).astype(F32)
    spread_v = jnp.logical_and(lax.rem(lane_v, own) == iota((own, lanes), 0), lane_v < own * part).astype(F32)
    none_e, none_v = jnp.zeros_like(spread_e), jnp.zeros_like(spread_v)
    spread = jnp.concatenate(
        [jnp.concatenate([none_v, none_v, spread_v], axis=1)]
        + [jnp.concatenate([spread_e, none_e, none_e], axis=1)] * 3
        + [jnp.concatenate([none_e, spread_e, none_e], axis=1)],
        axis=0,
    ).astype(BF16)

    def add_up(block, slope):
        sums = [jnp.zeros((SUB, lanes), F32)] * 4
        for t in range(steps):
            at = pl.ds(pl.multiple_of(block * rows + t * SUB, SUB), SUB)
            dose = dose_ref[at, :]
            moment = jnp.exp(shift_ref[at, :] if slope is None else shift_ref[at, :] + slope * dose)
            weight_ref[at, :] = moment
            for k in range(4):
                sums[k] = sums[k] + moment
                if k < 3:
                    moment = moment * dose
        for k in range(4):
            totals[pl.ds(pl.multiple_of(block * SUB, SUB), SUB), pl.ds(k * lanes, lanes)] = sums[k]

    def expand(slot, values):
        at = pl.ds(pl.multiple_of(slot * rows, rows), rows)
        doses, samples, events = values[:own], values[own : own + part], values[own + part :]
        mixed = jnp.concatenate([doses, *thirds(samples), events], axis=0)
        mixed = transposed_dot(mixed.astype(BF16), spread)
        shift_ref[at, :] = mixed[:, :lanes]
        mark_ref[at, :] = mixed[:, lanes : 2 * lanes]
        dose_ref[at, :] = mixed[:, 2 * lanes :]
        add_up(slot, None)

    expand(me, send[me])

    @pl.loop(1, n)
    def _(step):
        slot = peer(n - step)
        copy(slot, slot).wait_recv()
        expand(slot, recv[slot])

    blocks = n * SUB
    after = (iota((blocks, blocks), 1) > iota((blocks, blocks), 0)).astype(F32).astype(BF16)
    effect = jnp.zeros((1, lanes), F32)
    zscore = effect
    for sweep in range(ITERS):
        if sweep:
            slope = jnp.broadcast_to(effect, (SUB, lanes))

            def again(block, _):
                add_up(block, slope)
                return 0

            lax.fori_loop(0, n, again, 0, unroll=2)
        parts = [
            jnp.dot(after, part.astype(BF16), preferred_element_type=F32) for part in thirds(totals[...])
        ]
        carries[...] = (parts[0] + parts[1]) + parts[2]

        def add_terms(block, sums):
            score, information, skewness = sums
            here = pl.ds(pl.multiple_of(block * SUB, SUB), SUB)
            suffix = [carries[here, pl.ds(k * lanes, lanes)] for k in range(4)]
            for t in reversed(range(steps)):
                at = pl.ds(pl.multiple_of(block * rows + t * SUB, SUB), SUB)
                dose = dose_ref[at, :]
                mark = mark_ref[at, :]
                moment = weight_ref[at, :]
                for k in range(4):
                    suffix[k] = suffix[k] + moment
                    if k < 3:
                        moment = moment * dose
                inverse = 1.0 / suffix[0]
                first = suffix[1] * inverse
                second = suffix[2] * inverse
                third = suffix[3] * inverse
                spread = second - first * first
                score = score + mark * (dose - first)
                information = information + mark * spread
                skewness = skewness + mark * (third - first * (second + (spread + spread)))
            return score, information, skewness

        zero = jnp.zeros((SUB, lanes), F32)
        sums = lax.fori_loop(0, n, add_terms, (zero, zero, zero), unroll=2)
        score, information, skewness = (jnp.sum(x, axis=0, keepdims=True) for x in sums)
        effect = effect + (score + 0.5 * skewness / information) / information
        zscore = effect * jnp.sqrt(information)

    rsend[0:1, :] = effect
    rsend[1:2, :] = zscore

    @pl.loop(1, n)
    def _(step):
        rcopy(peer(step), me).start()

    rrecv[me] = rsend[...]

    @pl.loop(1, n)
    def _(step):
        copy(peer(step), me).wait_send()

    @pl.loop(1, n)
    def _(step):
        rcopy(peer(step), peer(step)).wait_recv()

    out_ref[...] = rrecv[...]

    @pl.loop(1, n)
    def _(step):
        rcopy(peer(step), me).wait_send()


def unfold(n, held, effect_ref, zscore_ref):
    endpoints, variants = effect_ref.shape
    part = endpoints // 2
    own = variants * 2 // n
    lanes = held.shape[2]
    owner = lax.div(iota((part, lanes), 1), own) == iota((part, lanes), 0)
    fold = jnp.logical_and(
        lax.rem(iota((lanes, variants), 0), own) == lax.rem(iota((lanes, variants), 1), own),
        iota((lanes, variants), 0) < own * part,
    ).astype(F32).astype(BF16)
    column = lax.div(iota((endpoints, variants), 1), own)
    for which, out in enumerate((effect_ref, zscore_ref)):
        tall = jnp.concatenate([jnp.where(owner, held[k, which : which + 1, :], 0.0) for k in range(n)], axis=0)
        parts = [jnp.dot(third.astype(BF16), fold, preferred_element_type=F32) for third in thirds(tall)]
        tall = (parts[0] + parts[1]) + parts[2]
        result = jnp.zeros((endpoints, variants), F32)
        for c in range(n // 2):
            result = jnp.where(column == c, tall[c * endpoints : (c + 1) * endpoints], result)
        out[...] = result


def solution(mesh):
    n = mesh.shape["smp"]

    def body(dosage, flags, events, offsets):
        rows, columns = dosage.shape
        endpoints = offsets.shape[1]
        variants = flags.shape[0]
        own = variants * 2 // n
        part = endpoints // 2
        lanes = -(-own * part // 128) * 128
        out = jax.ShapeDtypeStruct((endpoints, variants), F32)
        held = pl.pallas_call(
            functools.partial(kernel, n),
            out_shape=jax.ShapeDtypeStruct((n, 2, lanes), F32),
            in_specs=[pl.BlockSpec(memory_space=pl.ANY)] * 4,
            out_specs=pl.BlockSpec(memory_space=pltpu.VMEM),
            scratch_shapes=[
                pltpu.VMEM((1, variants), jnp.int32),
                pltpu.VMEM((rows, columns), BF16),
                pltpu.VMEM((endpoints, rows), F32),
                pltpu.VMEM((endpoints, rows), jnp.int32),
                pltpu.VMEM((n, own + 2 * part, rows), F32),
                pltpu.VMEM((n, own + 2 * part, rows), F32),
                pltpu.VMEM((n * rows, lanes), F32),
                pltpu.VMEM((n * rows, lanes), F32),
                pltpu.VMEM((n * rows, lanes), F32),
                pltpu.VMEM((n * rows, lanes), F32),
                pltpu.VMEM((n * SUB, 4 * lanes), F32),
                pltpu.VMEM((n * SUB, 4 * lanes), F32),
                pltpu.VMEM((2, lanes), F32),
                pltpu.VMEM((n, 2, lanes), F32),
                pltpu.SemaphoreType.DMA((4,)),
            ]
            + [pltpu.SemaphoreType.DMA((n,))] * 4,
            compiler_params=pltpu.CompilerParams(collective_id=0, has_side_effects=True),
        )(flags.reshape(1, variants), dosage, offsets.T, events.T)
        return pl.pallas_call(
            functools.partial(unfold, n),
            out_shape=(out, out),
            in_specs=[pl.BlockSpec(memory_space=pltpu.VMEM)],
            out_specs=[pl.BlockSpec(memory_space=pltpu.VMEM)] * 2,
        )(held)

    return jax.shard_map(
        body,
        mesh=mesh,
        in_specs=(P("smp", "grp"), P("grp"), P("smp", "grp"), P("smp", "grp")),
        out_specs=(P(None, "grp"), P(None, "grp")),
        check_vma=False,
    )
```

```python
import functools

import jax
import jax.numpy as jnp
from jax import lax
from jax.experimental import pallas as pl
from jax.experimental.pallas import tpu as pltpu
from jax.sharding import PartitionSpec as P

ITERS = 3
SUB = 8
GROUP = 5
MESH = pl.DeviceIdType.MESH
F32 = jnp.float32
BF16 = jnp.bfloat16


def thirds(x):
    high = x.astype(BF16).astype(F32)
    rest = x - high
    middle = rest.astype(BF16).astype(F32)
    return high, middle, rest - middle


def transposed_dot(a, b):
    return lax.dot_general(a, b, (((0,), (0,)), ((), ())), preferred_element_type=F32)


def iota(shape, dim):
    return lax.broadcasted_iota(jnp.int32, shape, dim)


def kernel(
    n, flags_hbm, dosage_hbm, offsets_hbm, events_hbm, out_ref,
    flags_ref, dosage_ref, offsets_ref, events_ref,
    send, recv, dose_ref, shift_ref, mark_ref, weight_ref, totals, carries, rsend, rrecv,
    load_sem, send_sem, recv_sem, rsend_sem, rrecv_sem,
):
    me = lax.axis_index("smp")
    rows, columns = dosage_ref.shape
    endpoints = offsets_ref.shape[0]
    part = endpoints // 2
    variants = flags_ref.shape[1]
    own = variants * 2 // n
    lanes = dose_ref.shape[1]
    steps = rows // SUB

    loads = [
        pltpu.make_async_copy(src, dst, load_sem.at[at])
        for at, (src, dst) in enumerate(
            ((flags_hbm, flags_ref), (dosage_hbm, dosage_ref), (offsets_hbm, offsets_ref), (events_hbm, events_ref))
        )
    ]
    for load in loads:
        load.start()

    barrier = pltpu.get_barrier_semaphore()

    def peer(step):
        return lax.rem(me + step, n)

    @pl.loop(1, n)
    def _(step):
        pl.semaphore_signal(barrier, inc=1, device_id={"smp": peer(step)}, device_id_type=MESH)

    line = iota((rows, rows), 1)
    order = (iota((rows, rows), 0) == lax.rem(line, SUB) * steps + lax.div(line, SUB)).astype(F32).astype(BF16)

    loads[2].wait()
    loads[3].wait()
    four = jnp.concatenate([*thirds(offsets_ref[...]), events_ref[...].astype(F32)], axis=0)
    four = jnp.dot(four.astype(BF16), order, preferred_element_type=F32)
    high, middle, low, events = (four[k * endpoints : (k + 1) * endpoints] for k in range(4))
    offsets = (high + middle) + low
    for k in range(n):
        for at, values in ((own, offsets), (own + part, events)):
            send[k, pl.ds(at, part), :] = values[k % 2 * part : (k % 2 + 1) * part]

    loads[0].wait()
    chosen = (iota((columns, variants), 0) == flags_ref[...]).astype(F32).astype(BF16)
    loads[1].wait()
    genotype = jnp.dot(dosage_ref[...], chosen, preferred_element_type=F32).astype(BF16)
    genotype = transposed_dot(genotype, order)
    for k in range(n):
        send[k, pl.ds(0, own), :] = genotype[k // 2 * own : (k // 2 + 1) * own]

    pl.semaphore_wait(barrier, n - 1)

    def copy(at, slot):
        return pltpu.make_async_remote_copy(
            src_ref=send.at[at], dst_ref=recv.at[slot], send_sem=send_sem.at[at], recv_sem=recv_sem.at[slot],
            device_id={"smp": at}, device_id_type=MESH,
        )

    def rcopy(at, slot):
        return pltpu.make_async_remote_copy(
            src_ref=rsend, dst_ref=rrecv.at[slot], send_sem=rsend_sem.at[at], recv_sem=rrecv_sem.at[slot],
            device_id={"smp": at}, device_id_type=MESH,
        )

    @pl.loop(1, n)
    def _(step):
        copy(peer(lax.rem(step + n // 2 - 2, n - 1) + 1), me).start()

    lane_e = iota((part, lanes), 1)
    lane_v = iota((own, lanes), 1)
    spread_e = (lax.div(lane_e, own) == iota((part, lanes), 0)).astype(F32)
    spread_v = jnp.logical_and(lax.rem(lane_v, own) == iota((own, lanes), 0), lane_v < own * part).astype(F32)
    none_e, none_v = jnp.zeros_like(spread_e), jnp.zeros_like(spread_v)
    spread = jnp.concatenate(
        [jnp.concatenate([none_v, none_v, spread_v], axis=1)]
        + [jnp.concatenate([spread_e, none_e, none_e], axis=1)] * 3
        + [jnp.concatenate([none_e, spread_e, none_e], axis=1)],
        axis=0,
    ).astype(BF16)

    def keep(block, sums):
        for k in range(4):
            totals[pl.ds(pl.multiple_of(block * SUB, SUB), SUB), pl.ds(k * lanes, lanes)] = sums[k]

    def add_up(block, slope):
        sums = [jnp.zeros((SUB, lanes), F32)] * 4
        for t in range(steps):
            at = pl.ds(pl.multiple_of(block * rows + t * SUB, SUB), SUB)
            dose = dose_ref[at, :]
            moment = jnp.exp(shift_ref[at, :] + slope * dose)
            weight_ref[at, :] = moment
            for k in range(4):
                sums[k] = sums[k] + moment
                if k < 3:
                    moment = moment * dose
        keep(block, sums)

    def expand(slots, pieces):
        mixed = []
        for values in pieces:
            doses, samples, events = values[:own], values[own : own + part], values[own + part :]
            tall = jnp.concatenate([doses, *thirds(samples), events], axis=0)
            mixed.append(transposed_dot(tall.astype(BF16), spread))
        for slot, values in zip(slots, mixed):
            at = pl.ds(pl.multiple_of(slot * rows, rows), rows)
            shifts, doses = values[:, :lanes], values[:, 2 * lanes :]
            shift_ref[at, :] = shifts
            mark_ref[at, :] = values[:, lanes : 2 * lanes]
            dose_ref[at, :] = doses
            moment = jnp.exp(shifts)
            weight_ref[at, :] = moment
            sums = []
            for k in range(4):
                sums.append(jnp.sum(moment.reshape(steps, SUB, lanes), axis=0))
                if k < 3:
                    moment = moment * doses
            keep(slot, sums)

    expand([me], [send[me]])
    group = max(size for size in range(1, GROUP + 1) if (n - 1) % size == 0)

    @pl.loop(0, (n - 1) // group)
    def _(step):
        slots = [peer(n - 1 - lax.rem(step * group + at + n // 2 - 1, n - 1)) for at in range(group)]
        for slot in slots:
            copy(slot, slot).wait_recv()
        expand(slots, [recv[slot] for slot in slots])

    blocks = n * SUB
    after = (iota((blocks, blocks), 1) > iota((blocks, blocks), 0)).astype(F32).astype(BF16)
    effect = jnp.zeros((1, lanes), F32)
    zscore = effect
    for sweep in range(ITERS):
        if sweep:
            slope = jnp.broadcast_to(effect, (SUB, lanes))

            def again(block, _):
                add_up(block, slope)
                return 0

            lax.fori_loop(0, n, again, 0, unroll=2)
        parts = [
            jnp.dot(after, part.astype(BF16), preferred_element_type=F32) for part in thirds(totals[...])
        ]
        carries[...] = (parts[0] + parts[1]) + parts[2]

        def add_terms(block, sums):
            score, information, skewness = sums
            here = pl.ds(pl.multiple_of(block * SUB, SUB), SUB)
            suffix = [carries[here, pl.ds(k * lanes, lanes)] for k in range(4)]
            for t in reversed(range(steps)):
                at = pl.ds(pl.multiple_of(block * rows + t * SUB, SUB), SUB)
                dose = dose_ref[at, :]
                mark = mark_ref[at, :]
                moment = weight_ref[at, :]
                for k in range(4):
                    suffix[k] = suffix[k] + moment
                    if k < 3:
                        moment = moment * dose
                inverse = 1.0 / suffix[0]
                first = suffix[1] * inverse
                second = suffix[2] * inverse
                third = suffix[3] * inverse
                spread = second - first * first
                score = score + mark * (dose - first)
                information = information + mark * spread
                skewness = skewness + mark * (third - first * (second + (spread + spread)))
            return score, information, skewness

        zero = jnp.zeros((SUB, lanes), F32)
        sums = lax.fori_loop(0, n, add_terms, (zero, zero, zero), unroll=2)
        score, information, skewness = (jnp.sum(x, axis=0, keepdims=True) for x in sums)
        effect = effect + (score + 0.5 * skewness / information) / information
        zscore = effect * jnp.sqrt(information)

    rsend[0:1, :] = effect
    rsend[1:2, :] = zscore

    @pl.loop(1, n)
    def _(step):
        rcopy(peer(step), me).start()

    rrecv[me] = rsend[...]

    @pl.loop(1, n)
    def _(step):
        copy(peer(step), me).wait_send()

    @pl.loop(1, n)
    def _(step):
        rcopy(peer(step), peer(step)).wait_recv()

    out_ref[...] = rrecv[...]

    @pl.loop(1, n)
    def _(step):
        rcopy(peer(step), me).wait_send()


def unfold(n, held, effect_ref, zscore_ref):
    endpoints, variants = effect_ref.shape
    part = endpoints // 2
    own = variants * 2 // n
    lanes = held.shape[2]
    owner = lax.div(iota((part, lanes), 1), own) == iota((part, lanes), 0)
    fold = jnp.logical_and(
        lax.rem(iota((lanes, variants), 0), own) == lax.rem(iota((lanes, variants), 1), own),
        iota((lanes, variants), 0) < own * part,
    ).astype(F32).astype(BF16)
    column = lax.div(iota((endpoints, variants), 1), own)
    for which, out in enumerate((effect_ref, zscore_ref)):
        tall = jnp.concatenate([jnp.where(owner, held[k, which : which + 1, :], 0.0) for k in range(n)], axis=0)
        parts = [jnp.dot(third.astype(BF16), fold, preferred_element_type=F32) for third in thirds(tall)]
        tall = (parts[0] + parts[1]) + parts[2]
        result = jnp.zeros((endpoints, variants), F32)
        for c in range(n // 2):
            result = jnp.where(column == c, tall[c * endpoints : (c + 1) * endpoints], result)
        out[...] = result


def solution(mesh):
    n = mesh.shape["smp"]

    def body(dosage, flags, events, offsets):
        rows, columns = dosage.shape
        endpoints = offsets.shape[1]
        variants = flags.shape[0]
        own = variants * 2 // n
        part = endpoints // 2
        lanes = -(-own * part // 128) * 128
        out = jax.ShapeDtypeStruct((endpoints, variants), F32)
        held = pl.pallas_call(
            functools.partial(kernel, n),
            out_shape=jax.ShapeDtypeStruct((n, 2, lanes), F32),
            in_specs=[pl.BlockSpec(memory_space=pl.ANY)] * 4,
            out_specs=pl.BlockSpec(memory_space=pltpu.VMEM),
            scratch_shapes=[
                pltpu.VMEM((1, variants), jnp.int32),
                pltpu.VMEM((rows, columns), BF16),
                pltpu.VMEM((endpoints, rows), F32),
                pltpu.VMEM((endpoints, rows), jnp.int32),
                pltpu.VMEM((n, own + 2 * part, rows), F32),
                pltpu.VMEM((n, own + 2 * part, rows), F32),
                pltpu.VMEM((n * rows, lanes), F32),
                pltpu.VMEM((n * rows, lanes), F32),
                pltpu.VMEM((n * rows, lanes), F32),
                pltpu.VMEM((n * rows, lanes), F32),
                pltpu.VMEM((n * SUB, 4 * lanes), F32),
                pltpu.VMEM((n * SUB, 4 * lanes), F32),
                pltpu.VMEM((2, lanes), F32),
                pltpu.VMEM((n, 2, lanes), F32),
                pltpu.SemaphoreType.DMA((4,)),
            ]
            + [pltpu.SemaphoreType.DMA((n,))] * 4,
            compiler_params=pltpu.CompilerParams(collective_id=0, has_side_effects=True),
        )(flags.reshape(1, variants), dosage, offsets.T, events.T)
        return pl.pallas_call(
            functools.partial(unfold, n),
            out_shape=(out, out),
            in_specs=[pl.BlockSpec(memory_space=pltpu.VMEM)],
            out_specs=[pl.BlockSpec(memory_space=pltpu.VMEM)] * 2,
        )(held)

    return jax.shard_map(
        body,
        mesh=mesh,
        in_specs=(P("smp", "grp"), P("grp"), P("smp", "grp"), P("smp", "grp")),
        out_specs=(P(None, "grp"), P(None, "grp")),
        check_vma=False,
    )
```
